512 devices in a mesh: head: 8 (over y, core), frame: 64 (over x, z).
Axes of the slice: x: 4, y: 4, z: 16, core: 2. Of those that a mesh axis runs over, the one named last changes fastest.
Arguments:
- queries: bfloat16 [65536, 16, 128], P(('frame', 'head')), may hold values from -30 to 30
- keys: bfloat16 [65536, 16, 128], P(('frame', 'head')), may hold values from -4 to 4
- values: bfloat16 [65536, 16, 128], P(('frame', 'head')), may hold values from -24 to 24
- block_mask: int32 [64, 16, 16], replicated, may hold values from 0 to 1, as said below
- strides: int32 [64], replicated, may hold values from 1 to 16, as said below
- offsets: int32 [64], replicated, may hold values from 0 to 15
Outputs:
- attended: bfloat16 [65536, 16, 128], P(('frame', 'head'))
The draws below stay inside these ranges and needn't reach their ends.
Inputs may be any that keep to these rules, and one draw needn't show every extreme that they name: Every diagonal entry block_mask[i, b, b] is 1. strides[0] is 1, strides[1] is 4, 8 or 16, and every later entry is 8 or 16.
All inputs are finite; a program needn't handle non-finite values.
Results may differ from the reference program's by a relative error of at most 0.0043.
Values may be sent and summed in bfloat16 or wider, within the bound.
No kernel may reach another device: no remote copies, remote signals or barrier semaphores. Data moves between devices by JAX's collectives and lax.ppermute only.
A program may use at most 64 MiB of HBM per device.

```python
import jax
import jax.numpy as jnp
from jax import lax

HD = 128
HEADS = 16
BLOCK = 64
TPF = 1024
FRAMES = 64
TOKENS = 65536


def integer_tables(key):
    frame_blocks = TPF // BLOCK
    offsets = jax.random.randint(jax.random.fold_in(key, 11), (FRAMES,), 0, frame_blocks)
    levels = jax.random.randint(jax.random.fold_in(key, 12), (FRAMES, 1, 1), 1, 8)
    coins = jax.random.randint(jax.random.fold_in(key, 13), (FRAMES, frame_blocks, frame_blocks), 0, 8)
    full_rows = jax.random.randint(jax.random.fold_in(key, 14), (FRAMES,), 0, frame_blocks)
    row_ids = jnp.arange(frame_blocks)[None, :, None]
    col_ids = jnp.arange(frame_blocks)[None, None, :]
    block_mask = ((coins < levels) | (row_ids == col_ids) | (row_ids == full_rows[:, None, None])).astype(jnp.int32)
    first_pick = jax.random.randint(jax.random.fold_in(key, 15), (), 0, 3)
    later_picks = jax.random.randint(jax.random.fold_in(key, 16), (FRAMES,), 0, 2)
    first_value = jnp.where(first_pick == 0, frame_blocks // 4, jnp.where(first_pick == 1, frame_blocks // 2, frame_blocks))
    later_values = jnp.where(later_picks == 0, frame_blocks // 2, frame_blocks)
    distances = jnp.arange(FRAMES)
    strides = jnp.where(distances == 0, 1, jnp.where(distances == 1, first_value, later_values)).astype(jnp.int32)
    return (offsets.astype(jnp.int32), block_mask, strides)


def attention_inputs(key):
    frame_blocks = TPF // BLOCK
    layout = (FRAMES, frame_blocks, BLOCK, HEADS, HD)
    query_draw = jnp.clip(jax.random.normal(jax.random.fold_in(key, 21), layout, jnp.float32), -4.0, 4.0)
    key_draw = jnp.clip(jax.random.normal(jax.random.fold_in(key, 22), layout, jnp.float32), -4.0, 4.0)
    shape = (FRAMES * TPF, HEADS, HD)
    return (query_draw.reshape(shape), key_draw.reshape(shape))


def draw_queries(key, part):
    return attention_inputs(key)[0].astype(jnp.bfloat16)


def draw_keys(key, part):
    return attention_inputs(key)[1].astype(jnp.bfloat16)


def draw_block_mask(key, part):
    return integer_tables(key)[1]


def draw_strides(key, part):
    return integer_tables(key)[2]


def draw_offsets(key, part):
    return integer_tables(key)[0]


def level_of(rng, dims, pieces, smallest, top_value):
    def one(position, blocks):
        heights = jax.random.uniform(jax.random.fold_in(jax.random.fold_in(rng, 6), position), (blocks,), jnp.float32, smallest / len(pieces), top_value / len(pieces))
        return jnp.repeat(jnp.exp(heights), dims[position] // blocks).reshape((-1,) + (1,) * (len(dims) - position - 1))

    loudness = one(*pieces[0])
    for cut in pieces[1:]:
        loudness = loudness * one(*cut)
    return loudness


def centred(rng, extent, scale, reach, pieces=(), kind=jnp.bfloat16):
    gain = level_of(rng, extent, pieces, -0.22, 0.18) if pieces else 1.0
    drawn = jax.random.normal(rng, extent, jnp.float32) * scale * gain
    return jnp.minimum(jnp.maximum(drawn, -reach), reach).astype(kind)


def setup_inputs(seed: int = 0) -> dict:
    streams_of = jax.random.split(jax.random.key(seed), 7)
    return {
        "queries": draw_queries(jax.random.fold_in(streams_of[6], 71), 0),
        "keys": draw_keys(jax.random.fold_in(streams_of[6], 71), 0),
        "values": centred(streams_of[2], (TOKENS, HEADS, HD), 4.0, 24.0, ((0, 512),)),
        "block_mask": draw_block_mask(jax.random.fold_in(streams_of[6], 71), 0),
        "strides": draw_strides(jax.random.fold_in(streams_of[6], 71), 0),
        "offsets": draw_offsets(jax.random.fold_in(streams_of[6], 71), 0),
    }


masked_score = -1.0e30


def group_terms(query_blocks, key_rows, value_rows, keep_mask, score_scale):
    query_wide = query_blocks.astype(jnp.float32)
    key_wide = key_rows.astype(jnp.float32)
    scores = jnp.einsum("qahd,gnhd->hqagn", query_wide, key_wide) * score_scale
    allowed = keep_mask[None, :, None, :, :]
    scores = jnp.where(allowed, scores, masked_score)
    group_tops = jnp.max(scores, axis=4)
    weights = jnp.where(allowed, jnp.exp(scores - group_tops[..., None]), 0.0)
    group_totals = jnp.sum(weights, axis=4)
    rounded = lax.optimization_barrier(weights.astype(jnp.bfloat16)).astype(jnp.float32)
    group_sums = jnp.einsum("hqagn,gnhd->hqagd", rounded, value_rows.astype(jnp.float32))
    return group_tops, group_totals, group_sums


def reference(queries, keys, values, block_mask, strides, offsets):
    frame_blocks = TPF // BLOCK
    score_scale = HD ** -0.5
    layout = (FRAMES, frame_blocks, BLOCK, HEADS, HD)
    query_all = queries.reshape(layout)
    key_all = keys.reshape(layout)
    value_all = values.reshape(layout)
    frame_ids = jnp.arange(FRAMES, dtype=jnp.int32)
    anchors = (frame_blocks - offsets % frame_blocks) % frame_blocks
    anchor_keys = key_all[frame_ids, anchors]
    anchor_values = value_all[frame_ids, anchors]

    def one_frame(frame_index):
        query_blocks = query_all[frame_index]
        own_mask = block_mask[frame_index] == 1
        results = []
        keep_mask = jnp.repeat(own_mask, BLOCK, axis=1)[:, None, :]
        results.append(group_terms(query_blocks, key_all[frame_index].reshape(1, TPF, HEADS, HD),
                                   value_all[frame_index].reshape(1, TPF, HEADS, HD), keep_mask, score_scale))
        for distance in (1, 2, 3):
            spacing = frame_blocks // 4 if distance == 1 else frame_blocks // 2
            block_count = frame_blocks // spacing
            for direction in (1, -1):
                source_frame = frame_index - direction * distance
                valid = (source_frame >= 0) & (source_frame < FRAMES)
                clipped = jnp.clip(source_frame, 0, FRAMES - 1)
                chosen = (spacing - offsets[clipped] % spacing) % spacing + spacing * jnp.arange(block_count, dtype=jnp.int32)
                phase_ok = ((chosen + offsets[clipped]) % strides[distance]) == 0
                kept = valid & own_mask[:, chosen] & phase_ok[None, :]
                keep_mask = jnp.repeat(kept, BLOCK, axis=1)[:, None, :]
                chosen_keys = key_all[clipped][chosen].reshape(1, block_count * BLOCK, HEADS, HD)
                chosen_values = value_all[clipped][chosen].reshape(1, block_count * BLOCK, HEADS, HD)
                results.append(group_terms(query_blocks, chosen_keys, chosen_values, keep_mask, score_scale))
        distances = jnp.abs(frame_index - frame_ids)
        phase_ok = ((anchors + offsets) % strides[distances]) == 0
        kept = (distances >= 4)[None, :] & own_mask[:, anchors] & phase_ok[None, :]
        keep_mask = jnp.repeat(kept, BLOCK, axis=1).reshape(frame_blocks, FRAMES, BLOCK)
        results.append(group_terms(query_blocks, anchor_keys, anchor_values, keep_mask, score_scale))
        group_tops = jnp.concatenate([entry[0] for entry in results], axis=3)
        group_totals = jnp.concatenate([entry[1] for entry in results], axis=3)
        group_sums = jnp.concatenate([entry[2] for entry in results], axis=3)
        overall_top = jnp.max(group_tops, axis=3)
        factors = jnp.exp(group_tops - overall_top[..., None])
        denominator = jnp.sum(factors * group_totals, axis=3)
        numerator = jnp.sum(factors[..., None] * group_sums, axis=3)
        output = (numerator / denominator[..., None]).astype(jnp.bfloat16)
        return jnp.transpose(output, (1, 2, 0, 3))

    result = lax.map(one_frame, frame_ids)
    return result.reshape(FRAMES * TPF, HEADS, HD)
```

```python
import functools

import jax
import jax.numpy as jnp
from jax import lax
from jax.experimental import pallas as pl
from jax.experimental.pallas import tpu as pltpu
from jax.sharding import Mesh
from jax.sharding import PartitionSpec as P

masked_score = -1e30
log2_e = 1.4426950408889634
row_tile = 256


def attend_kernel(plan, first, last, block_rows, shifts, queries, bias, *refs):
    arrays = refs[: plan["arrays"]]
    refs = refs[plan["arrays"] :]
    if not first:
        top_in, total_in, sum_in = refs[:3]
        refs = refs[3:]
    outs, (key_buffer, value_buffer) = refs[:-2], refs[-2:]
    slot = pl.program_id(0)

    def fill(part):
        position = 0
        for which, kind, index in plan["pieces"]:
            source = arrays[which]
            if kind == "own":
                size = source.shape[0] * 0 + source.shape[1] * source.shape[3]
                if part == "slot":
                    shape = (size, source.shape[4])
                    key_buffer[position : position + size] = source[0, :, 0].reshape(shape)
                    value_buffer[position : position + size] = source[0, :, 1].reshape(shape)
            elif kind == "extra":
                size = block_rows
                if part == "slot":
                    shift, entry = index
                    place = (slot + shifts[shift]) & 3
                    key_buffer[position : position + size] = source[place, entry, 0]
                    value_buffer[position : position + size] = source[place, entry, 1]
            else:
                size = source.shape[0] * block_rows
                if part == "once":
                    shape = (size, source.shape[4])
                    key_buffer[position : position + size] = source[:, 0, 0].reshape(shape)
                    value_buffer[position : position + size] = source[:, 0, 1].reshape(shape)
            position += size

    @pl.when((slot == 0) & (pl.program_id(1) == 0))
    def _():
        fill("once")

    @pl.when(pl.program_id(1) == 0)
    def _():
        fill("slot")

    query_tile = queries[0]
    rows, head_dim = query_tile.shape
    factor = head_dim ** (-0.5) * log2_e
    scores = lax.dot_general(
        query_tile, key_buffer[...], (((1,), (1,)), ((), ())), preferred_element_type=jnp.float32
    )
    key_count = scores.shape[1]
    scores = scores.reshape(rows // block_rows, block_rows, key_count) + bias[0, 0][:, None, :]
    scores = scores.reshape(rows, key_count)
    top = jnp.max(scores, axis=1, keepdims=True)
    if not first:
        top = jnp.maximum(top, top_in[0][:, :1])
    weights = jnp.exp2((scores - top) * factor)
    total = weights[:, :128]
    for place in range(128, key_count, 128):
        total = total + weights[:, place : place + 128]
    summed = jnp.dot(
        weights.astype(jnp.bfloat16), value_buffer[...], preferred_element_type=jnp.float32
    )
    if not first:
        shrink = jnp.exp2((top_in[0] - top) * factor)
        total = total + shrink * total_in[0]
        summed = summed + shrink * sum_in[0]
    if last:
        outs[0][0] = (summed / jnp.sum(total, axis=1, keepdims=True)).astype(jnp.bfloat16)
    else:
        outs[0][0] = jnp.broadcast_to(top, (rows, 128))
        outs[1][0] = total
        outs[2][0] = summed


def attend(queries, bias, shifts, arrays, pieces, state, last, block_rows):
    slots, slot_rows, head_dim = queries.shape
    key_count = bias.shape[-1]
    tiles = slot_rows // row_tile
    tile_spec = pl.BlockSpec((1, row_tile, head_dim), lambda s, t, *_: (s, t, 0))
    specs = [tile_spec, pl.BlockSpec((1, 1) + bias.shape[2:], lambda s, t, *_: (s, t, 0, 0))]
    for which, array in enumerate(arrays):
        own = any(kind == "own" for w, kind, index in pieces if w == which)
        if own:
            specs.append(pl.BlockSpec((1,) + array.shape[1:], lambda s, t, *_: (s, 0, 0, 0, 0)))
        else:
            specs.append(pl.BlockSpec(array.shape, lambda s, t, *_: (0, 0, 0, 0, 0)))
    state_shape = jax.ShapeDtypeStruct((slots, slot_rows, 128), jnp.float32)
    if last:
        out_shape = [jax.ShapeDtypeStruct(queries.shape, jnp.bfloat16)]
    else:
        out_shape = [state_shape] * 3
    carried = [] if state is None else list(state)
    specs += [tile_spec] * len(carried)
    plan = {"arrays": len(arrays), "pieces": pieces}
    flops = 4 * slots * slot_rows * key_count * head_dim
    return pl.pallas_call(
        functools.partial(attend_kernel, plan, state is None, last, block_rows),
        out_shape=out_shape,
        grid_spec=pltpu.PrefetchScalarGridSpec(
            num_scalar_prefetch=1,
            grid=(slots, tiles),
            in_specs=specs,
            out_specs=[tile_spec] * len(out_shape),
            scratch_shapes=[
                pltpu.VMEM((key_count, head_dim), jnp.bfloat16),
                pltpu.VMEM((key_count, head_dim), jnp.bfloat16),
            ],
        ),
        cost_estimate=pl.CostEstimate(
            flops=flops,
            transcendentals=slots * slot_rows * key_count,
            bytes_accessed=8 * 1024 * 1024,
        ),
    )(shifts, queries, bias, *arrays, *carried)


def local(queries, keys, values, block_mask, strides, offsets):
    core = lax.axis_index("core")
    depth = lax.axis_index("z")
    cores, depths, planes = lax.axis_size("core"), lax.axis_size("z"), lax.axis_size("x")
    frame_total, frame_blocks = block_mask.shape[0], block_mask.shape[1]
    local_rows, heads, head_dim = queries.shape
    rows_y = lax.axis_size("y")
    block_rows = local_rows * rows_y * cores // frame_blocks
    swap = [(0, 1), (1, 0)]
    onward = [(z, (z + 1) % depths) for z in range(depths)]
    onward += [(depths + z, depths + (z - 1) % depths) for z in range(depths)]

    packed = jnp.stack([jnp.transpose(keys, (1, 0, 2)), jnp.transpose(values, (1, 0, 2))], axis=1)
    own_pair = lax.all_to_all(packed, ("x", "y"), split_axis=0, concat_axis=0, tiled=True)
    own_pair = own_pair.reshape(planes, rows_y, 2, local_rows, head_dim)
    partner_pair = lax.ppermute(own_pair, "core", swap)
    head_queries = lax.all_to_all(
        jnp.transpose(queries, (1, 0, 2)), ("x", "y"), split_axis=0, concat_axis=0, tiled=True
    )
    head_queries = head_queries.reshape(planes, rows_y * local_rows, head_dim)

    anchors = (frame_blocks - offsets % frame_blocks) % frame_blocks
    slot_ids = jnp.arange(planes, dtype=jnp.int32)
    own_frames = slot_ids * depths + depth
    own_mask = lax.dynamic_index_in_dim(
        block_mask.reshape(planes, depths, frame_blocks, frame_blocks), depth, 1, keepdims=False
    )
    split_mask = own_mask.reshape(planes, rows_y, cores, -1, frame_blocks)
    query_mask = lax.dynamic_index_in_dim(split_mask, core, 2, keepdims=False)
    query_mask = query_mask.reshape(planes, -1, frame_blocks).astype(jnp.float32)
    signs = (2 * core - 1, 1 - 2 * core)

    def own_columns():
        shape = (rows_y, local_rows // block_rows)
        columns = []
        for side in (core, 1 - core):
            place = jnp.arange(rows_y)[:, None] * (frame_blocks // rows_y)
            place = place + side * shape[1] + jnp.arange(shape[1])[None, :]
            columns.append(jnp.broadcast_to(place.reshape(1, -1), (planes, shape[0] * shape[1])))
        columns = jnp.concatenate(columns, axis=1)
        return columns, jnp.ones(columns.shape, jnp.bool_)

    def extra_column(sign, distance, part):
        source = own_frames + sign * distance
        valid = (source >= 0) & (source < frame_total)
        column = (anchors[jnp.clip(source, 0, frame_total - 1)] + 4 * part) % frame_blocks
        kept = (4 * part) % strides[distance] == 0
        return column[:, None], (valid & kept)[:, None]

    def anchor_columns(source_depth):
        sources = slot_ids * depths + source_depth % depths
        column = jnp.broadcast_to(anchors[sources][None, :], (planes, planes))
        return column, sources[None, :] != own_frames[:, None]

    def bias_of(columns):
        column = jnp.concatenate([entry[0] for entry in columns], axis=1)
        valid = jnp.concatenate([entry[1] for entry in columns], axis=1)
        code = jnp.where(valid, column, -1).astype(jnp.int32)
        code = jnp.repeat(code, block_rows, axis=1)
        chosen = jnp.arange(frame_blocks, dtype=jnp.int32)[None, :, None] == code[:, None, :]
        kept = jnp.einsum("sbc,scn->sbn", query_mask, chosen.astype(jnp.float32))
        bias = jnp.where(kept > 0.5, 0.0, masked_score)
        tiles = rows_y * local_rows // row_tile
        return bias.reshape(planes, tiles, -1, bias.shape[-1])

    residue = anchors[own_frames] % 4
    both = jnp.stack([own_pair, partner_pair]).reshape(-1, block_rows, head_dim)
    side = (residue // 2) ^ core
    halves = local_rows // block_rows
    parts = jnp.arange(4, dtype=jnp.int32)
    row_y = (anchors[own_frames][:, None] // 4 + parts[None, :]) % 4
    index = (side[:, None] * planes + slot_ids[:, None]) * rows_y + row_y
    index = index[:, :, None] * 2 + jnp.arange(2, dtype=jnp.int32)
    index = index * halves + (residue % 2)[:, None, None]
    candidates = jnp.take(both, index.reshape(-1), axis=0).reshape(
        planes, 4, 2, block_rows, head_dim
    )

    carried = candidates
    mine, other = {}, {}
    for step in range(1, depths // 2 + 1):
        carried = lax.ppermute(carried, ("core", "z"), onward)
        mine[step] = carried
        if step < depths // 2:
            other[step] = lax.ppermute(carried, "core", swap)
        if step == 1:
            carried = jnp.stack([carried[:, 0], carried[:, 2]], axis=1)
        elif step == 3:
            carried = carried[:, :1]

    near = (1, 2, 3)
    shifts = jnp.stack([(depth + sign * k) // depths for sign in signs for k in near])
    shifts = (shifts + planes).astype(jnp.int32)

    state = attend(
        head_queries,
        bias_of([own_columns()]),
        shifts,
        [own_pair, partner_pair],
        [(0, "own", None), (1, "own", None)],
        None,
        False,
        block_rows,
    )
    arrays = [candidates[:, :1]]
    pieces = [(0, "anchor", None)]
    columns = [anchor_columns(depth)]
    for sign, held, first_shift in ((signs[0], mine, 0), (signs[1], other, 3)):
        for k in near:
            arrays.append(held[k])
            which = len(arrays) - 1
            pieces.append((which, "anchor", None))
            columns.append(anchor_columns(depth + sign * k + depths))
            for entry, part in ((1, 1), (2, 2), (3, 3)) if k == 1 else ((1, 2),):
                pieces.append((which, "extra", (first_shift + k - 1, entry)))
                columns.append(extra_column(sign, k, part))
    state = attend(
        head_queries, bias_of(columns), shifts, arrays, pieces, state, False, block_rows
    )
    for steps, last in (((4, 5, 6), False), ((7, 8), True)):
        arrays, columns = [], []
        for k in steps:
            arrays.append(mine[k])
            columns.append(anchor_columns(depth + signs[0] * k + depths))
            if k in other:
                arrays.append(other[k])
                columns.append(anchor_columns(depth + signs[1] * k + depths))
        pieces = [(which, "anchor", None) for which in range(len(arrays))]
        state = attend(
            head_queries, bias_of(columns), shifts, arrays, pieces, state, last, block_rows
        )

    output = state[0].reshape(planes * rows_y, local_rows, head_dim)
    output = lax.all_to_all(output, ("x", "y"), split_axis=0, concat_axis=0, tiled=True)
    return jnp.transpose(output, (1, 0, 2))


def solution(mesh):
    grid = Mesh(mesh.devices.reshape(4, 2, 4, 16), ("y", "core", "x", "z"))
    tokens = P(("x", "z", "y", "core"), None, None)
    return jax.shard_map(
        local,
        mesh=grid,
        in_specs=(tokens, tokens, tokens, P(), P(), P()),
        out_specs=tokens,
        check_vma=False,
    )
```

```python
import functools

import jax
import jax.numpy as jnp
import numpy as np
from jax import lax
from jax.experimental import pallas as pl
from jax.experimental.pallas import tpu as pltpu
from jax.sharding import Mesh
from jax.sharding import PartitionSpec as P


masked_score = -1e30
log2_e = 1.4426950408889634
row_tile = 256


def attend_kernel(plan, first, last, block_rows, shifts, queries, bias, *refs):
    arrays = refs[: plan["arrays"]]
    refs = refs[plan["arrays"] :]
    if not first:
        marks_in, sum_in = refs[:2]
        refs = refs[2:]
    outs, (key_buffer, value_buffer, score_buffer) = refs[:-3], refs[-3:]
    slot = pl.program_id(0)

    def fill(part):
        position = 0
        for which, kind, index in plan["pieces"]:
            source = arrays[which]
            head_dim = source.shape[4]
            if kind == "own":
                size = source.shape[1] * source.shape[3]
                if part == "slot":
                    shape = (size, head_dim)
                    key_buffer[position : position + size] = source[0, :, 0].reshape(shape)
                    value_buffer[position : position + size] = source[0, :, 1].reshape(shape)
            elif kind == "extra":
                size = block_rows
                if part == "slot":
                    shift, entry = index
                    place = (slot + shifts[shift]) & 3
                    key_buffer[position : position + size] = source[place, entry, 0]
                    value_buffer[position : position + size] = source[place, entry, 1]
            else:
                size = source.shape[0] * block_rows
                if part == "once":
                    shape = (size, head_dim)
                    key_buffer[position : position + size] = source[:, index, 0].reshape(shape)
                    value_buffer[position : position + size] = source[:, index, 1].reshape(shape)
            position += size
        spare = key_buffer.shape[0] - position
        if part == "once" and spare:
            key_buffer[position:] = jnp.zeros((spare, key_buffer.shape[1]), jnp.bfloat16)
            value_buffer[position:] = jnp.zeros((spare, key_buffer.shape[1]), jnp.bfloat16)

    @pl.when(slot == 0)
    def _():
        fill("once")

    if any(kind != "anchor" for _, kind, _ in plan["pieces"]):
        fill("slot")

    key_count, head_dim = key_buffer.shape
    factor = head_dim ** (-0.5) * log2_e
    groups = row_tile // block_rows
    chunks = [(at, min(256, key_count - at)) for at in range(0, key_count, 256)]

    for tile in range(queries.shape[1] // row_tile):
        rows = slice(tile * row_tile, (tile + 1) * row_tile)
        query_tile = queries[0, rows]
        highest = None
        for at, width in chunks:
            scores = lax.dot_general(
                query_tile,
                key_buffer[at : at + width],
                (((1,), (1,)), ((), ())),
                preferred_element_type=jnp.float32,
            )
            seen = bias[0, tile * groups : (tile + 1) * groups, at : at + width]
            scores = scores.reshape(groups, block_rows, width) + seen[:, None, :]
            scores = scores.reshape(row_tile, width)
            score_buffer[:, at : at + width] = scores
            for place in range(0, width, 128):
                part = scores[:, place : place + 128]
                highest = part if highest is None else jnp.maximum(highest, part)
        top = jnp.max(highest, axis=1, keepdims=True)
        if not first:
            top = jnp.maximum(top, marks_in[0, rows, :1])
        total = jnp.zeros((row_tile, 128), jnp.float32)
        summed = jnp.zeros((row_tile, head_dim), jnp.float32)
        for at, width in chunks:
            weights = jnp.exp2((score_buffer[:, at : at + width] - top) * factor)
            for place in range(0, width, 128):
                total = total + weights[:, place : place + 128]
            summed = summed + jnp.dot(
                weights.astype(jnp.bfloat16),
                value_buffer[at : at + width],
                preferred_element_type=jnp.float32,
            )
        total = jnp.sum(total, axis=1, keepdims=True)
        if not first:
            shrink = jnp.exp2((marks_in[0, rows, :1] - top) * factor)
            total = total + shrink * marks_in[0, rows, 127:]
            summed = summed + shrink * sum_in[0, rows]
        if last:
            outs[0][0, rows] = (summed / total).astype(jnp.bfloat16)
        else:
            lane = lax.broadcasted_iota(jnp.int32, (row_tile, 128), 1)
            outs[0][0, rows] = jnp.where(lane < 64, top, total)
            outs[1][0, rows] = summed


def attend(queries, bias, shifts, arrays, pieces, state, last, block_rows):
    slots, slot_rows, head_dim = queries.shape
    key_count = bias.shape[-1]
    slot_spec = pl.BlockSpec((1, slot_rows, head_dim), lambda s, *_: (s, 0, 0))
    specs = [slot_spec, pl.BlockSpec((1,) + bias.shape[1:], lambda s, *_: (s, 0, 0))]
    for which, array in enumerate(arrays):
        own = any(kind == "own" for w, kind, index in pieces if w == which)
        if own:
            specs.append(pl.BlockSpec((1,) + array.shape[1:], lambda s, *_: (s, 0, 0, 0, 0)))
        else:
            specs.append(pl.BlockSpec(array.shape, lambda s, *_: (0, 0, 0, 0, 0)))
    state_shape = jax.ShapeDtypeStruct((slots, slot_rows, 128), jnp.float32)
    if last:
        out_shape = [jax.ShapeDtypeStruct(queries.shape, jnp.bfloat16)]
    else:
        out_shape = [state_shape] * 2
    carried = [] if state is None else list(state)
    specs += [slot_spec] * len(carried)
    plan = {"arrays": len(arrays), "pieces": pieces}
    return pl.pallas_call(
        functools.partial(attend_kernel, plan, state is None, last, block_rows),
        out_shape=out_shape,
        grid_spec=pltpu.PrefetchScalarGridSpec(
            num_scalar_prefetch=1,
            grid=(slots,),
            in_specs=specs,
            out_specs=[slot_spec] * len(out_shape),
            scratch_shapes=[
                pltpu.VMEM((key_count, head_dim), jnp.bfloat16),
                pltpu.VMEM((key_count, head_dim), jnp.bfloat16),
                pltpu.VMEM((row_tile, key_count), jnp.float32),
            ],
        ),
        cost_estimate=pl.CostEstimate(
            flops=4 * slots * slot_rows * key_count * head_dim,
            transcendentals=slots * slot_rows * key_count,
            bytes_accessed=8 * 1024 * 1024,
        ),
    )(shifts, queries, bias, *arrays, *carried)


def after(value, *earlier):
    return lax.optimization_barrier((value,) + earlier)[0]


def local(queries, keys, values, block_mask, strides, offsets):
    core = lax.axis_index("core")
    plane = lax.axis_index("x")
    depth = lax.axis_index("z")
    cores, depths, planes = lax.axis_size("core"), lax.axis_size("z"), lax.axis_size("x")
    frame_total, frame_blocks = block_mask.shape[0], block_mask.shape[1]
    local_rows, _, head_dim = queries.shape
    rows_y = lax.axis_size("y")
    block_rows = local_rows * rows_y * cores // frame_blocks
    halves = local_rows // block_rows
    swap = [(0, 1), (1, 0)]

    def spread(packed):
        return lax.all_to_all(packed, ("x", "y"), split_axis=0, concat_axis=0, tiled=True)

    def onward(carried, distance):
        route = [(z, (z + distance) % depths) for z in range(depths)]
        route += [(depths + z, depths + (z - distance) % depths) for z in range(depths)]
        return lax.ppermute(carried, ("core", "z"), route)

    anchors = (frame_blocks - offsets % frame_blocks) % frame_blocks
    residue = lax.dynamic_index_in_dim(anchors, plane * depths + depth, keepdims=False) % 4
    packed = jnp.stack([jnp.transpose(keys, (1, 0, 2)), jnp.transpose(values, (1, 0, 2))], axis=1)
    block = lax.dynamic_slice_in_dim(packed, (residue % 2) * block_rows, block_rows, axis=2)
    block = jnp.where(residue // 2 == core, block, lax.ppermute(block, "core", swap))
    block = spread(block)

    slot_ids = jnp.arange(planes, dtype=jnp.int32)
    own_frames = slot_ids * depths + depth
    own_anchors = lax.dynamic_index_in_dim(
        anchors.reshape(planes, depths), depth, 1, keepdims=False
    )
    parts = jnp.arange(4, dtype=jnp.int32)
    parts = parts * 2 - 3 * (parts // 2)
    row_y = (own_anchors[:, None] // 4 + parts[None, :]) % 4
    index = (slot_ids[:, None] * rows_y + row_y).reshape(-1)
    held = jnp.take(block, index, axis=0).reshape(planes, 4, 2, block_rows, head_dim)

    head_queries = spread(after(jnp.transpose(queries, (1, 0, 2)), held))
    own_pair = spread(after(packed, head_queries))
    head_queries = head_queries.reshape(planes, rows_y * local_rows, head_dim)
    own_pair = own_pair.reshape(planes, rows_y, 2, local_rows, head_dim)
    partner_pair = lax.ppermute(own_pair, "core", swap)

    own_mask = lax.dynamic_index_in_dim(
        block_mask.reshape(planes, depths, frame_blocks, frame_blocks), depth, 1, keepdims=False
    )
    split_mask = own_mask.reshape(planes, rows_y, cores, halves, frame_blocks)
    query_mask = lax.dynamic_index_in_dim(split_mask, core, 2, keepdims=False)
    query_mask = query_mask.reshape(planes, -1, frame_blocks).astype(jnp.bfloat16)
    near_steps = lax.iota(jnp.int32, 6) % 3 + 1
    near_signs = (1 - 2 * (lax.iota(jnp.int32, 6) // 3)) * (2 * core - 1)
    shifts = (depth + near_signs * near_steps) // depths + planes

    calls, entries = [], []

    def begin():
        calls.append(([], [], [len(entries)]))

    def end():
        while len(entries) % 2:
            entries.append((3, 1, 0, 0, 0))
        calls[-1][2].append(len(entries))

    def anchor(which, entry, side, distance):
        calls[-1][1].append((which, "anchor", entry))
        entries.extend((2, side, distance, 0, place) for place in range(planes))

    def extra(which, entry, side, distance, part):
        shift = (0 if side == 1 else 3) + distance - 1
        calls[-1][1].append((which, "extra", (shift, entry)))
        entries.append((1, side, distance, part, 0))

    def own(which, partner):
        calls[-1][1].append((which, "own", None))
        spacing = frame_blocks // rows_y
        for y in range(rows_y):
            entries.extend((0, 1, 0, partner, spacing * y + j) for j in range(halves))

    def first_pieces(far, far_entry, near, near_entry, side):
        anchor(far, far_entry, side, 1)
        extra(near, near_entry, side, 1, 2)
        extra(near, near_entry + 1, side, 1, 1)
        extra(near, near_entry + 2, side, 1, 3)

    def second_pieces(far, far_entry, near, near_entry, side):
        anchor(far, far_entry, side, 2)
        anchor(far, far_entry + 1, side, 3)
        extra(near, near_entry, side, 2, 2)
        extra(near, near_entry + 1, side, 3, 2)

    begin()
    anchor(0, 0, 1, 0)
    first_pieces(1, 0, 2, 0, 1)
    end()
    begin()
    second_pieces(0, 0, 1, 0, 1)
    first_pieces(2, 0, 2, 1, -1)
    second_pieces(2, 4, 2, 6, -1)
    end()
    begin()
    own(0, 0)
    own(1, 1)
    for entry in range(3):
        anchor(2, entry, 1, 4 + entry)
    end()
    begin()
    for entry in range(2):
        anchor(0, entry, 1, 7 + entry)
    end()
    begin()
    for entry in range(4):
        anchor(0, entry, -1, 4 + entry)
    end()

    table = jnp.asarray(np.array(entries, np.int32).T)
    kind, side, distance, part, place = (table[row][None, :] for row in range(5))
    sign = (2 * core - 1) * side
    near = own_frames[:, None] + sign * distance
    far = place * depths + (depth + sign * distance + depths) % depths
    source = jnp.where(kind == 1, near, far)
    stride = jnp.where(distance == 1, strides[1], jnp.where(distance == 2, strides[2], strides[3]))
    fits = (near >= 0) & (near < frame_total) & ((4 * part) % stride == 0)
    valid = jnp.where(kind == 1, fits, source != own_frames[:, None])
    valid = (valid | (kind == 0)) & (kind != 3)
    every = jnp.arange(frame_total, dtype=jnp.int32)
    picked = jnp.where(source[:, :, None] == every, anchors, 0)
    column = (jnp.sum(picked, axis=2) + 4 * part) % frame_blocks
    column = jnp.where(kind == 0, place + halves * (core ^ part), column)
    code = jnp.repeat(jnp.where(valid, column, -1), block_rows, axis=1)
    chosen = jnp.arange(frame_blocks, dtype=jnp.int32)[None, :, None] == code[:, None, :]
    kept = jnp.einsum(
        "sbc,scn->sbn",
        query_mask,
        chosen.astype(jnp.bfloat16),
        preferred_element_type=jnp.float32,
    )
    bias = jnp.where(kept > 0.5, 0.0, masked_score)

    def run(number, arrays, state, last=False):
        pieces, (start, stop) = calls[number][1:]
        seen = bias[:, :, start * block_rows : stop * block_rows]
        return attend(
            head_queries, seen, shifts, arrays, pieces, state, last, block_rows
        )

    first = onward(held[:, :1], 1)
    near_first = onward(held[:, 1:], 1)
    second = onward(jnp.concatenate([held[:, :1], first], axis=1), 2)
    near_second = jnp.concatenate([held[:, 1:2], near_first[:, :1]], axis=1)
    near_second = onward(near_second, 2)
    third = onward(jnp.concatenate([first, second], axis=1), 3)
    fourth = onward(third[:, :2], 3)
    near = jnp.concatenate([first, near_first, second, near_second], axis=1)
    near_other = lax.ppermute(near, "core", swap)
    far_other = lax.ppermute(
        jnp.concatenate([third, fourth[:, :1]], axis=1), "core", swap
    )
    state = run(0, [held[:, :1], first, near_first], None)
    state = run(1, [second, near_second, near_other], state)
    state = run(2, [own_pair, partner_pair, third], state)
    state = run(3, [fourth], state)
    state = run(4, [far_other], state, last=True)

    output = state[0].reshape(planes * rows_y, local_rows, head_dim)
    return jnp.transpose(spread(output), (1, 0, 2))


def solution(mesh):
    grid = Mesh(mesh.devices.reshape(4, 2, 4, 16), ("y", "core", "x", "z"))
    tokens = P(("x", "z", "y", "core"), None, None)
    return jax.shard_map(
        local,
        mesh=grid,
        in_specs=(tokens, tokens, tokens, P(), P(), P()),
        out_specs=tokens,
        check_vma=False,
    )
```

```python
import functools

import jax
import jax.numpy as jnp
import numpy as np
from jax import lax
from jax.experimental import pallas as pl
from jax.experimental.pallas import tpu as pltpu
from jax.sharding import Mesh
from jax.sharding import PartitionSpec as P


masked_score = -1e30
log2_e = 1.4426950408889634
row_tile = 256


def attend_kernel(plan, first, last, block_rows, shifts, queries, bias, *refs):
    arrays = refs[: plan["arrays"]]
    refs = refs[plan["arrays"] :]
    if not first:
        marks_in, sum_in = refs[:2]
        refs = refs[2:]
    outs, (key_buffer, value_buffer, score_buffer) = refs[:-3], refs[-3:]
    slot = pl.program_id(0)

    def fill(part):
        position = 0
        for which, kind, index in plan["pieces"]:
            source = arrays[which]
            head_dim = source.shape[4]
            if kind == "own":
                size = source.shape[1] * source.shape[3]
                if part == "slot":
                    shape = (size, head_dim)
                    key_buffer[position : position + size] = source[0, :, 0].reshape(shape)
                    value_buffer[position : position + size] = source[0, :, 1].reshape(shape)
            elif kind == "extra":
                size = block_rows
                if part == "slot":
                    shift, entry = index
                    place = (slot + shifts[shift]) & 3
                    key_buffer[position : position + size] = source[place, entry, 0]
                    value_buffer[position : position + size] = source[place, entry, 1]
            else:
                size = source.shape[0] * block_rows
                if part == "once":
                    shape = (size, head_dim)
                    key_buffer[position : position + size] = source[:, index, 0].reshape(shape)
                    value_buffer[position : position + size] = source[:, index, 1].reshape(shape)
            position += size
        spare = key_buffer.shape[0] - position
        if part == "once" and spare:
            key_buffer[position:] = jnp.zeros((spare, key_buffer.shape[1]), jnp.bfloat16)
            value_buffer[position:] = jnp.zeros((spare, key_buffer.shape[1]), jnp.bfloat16)

    @pl.when(slot == 0)
    def _():
        fill("once")

    if any(kind != "anchor" for _, kind, _ in plan["pieces"]):
        fill("slot")

    key_count, head_dim = key_buffer.shape
    factor = head_dim ** (-0.5) * log2_e
    groups = row_tile // block_rows
    base = plan["base"]
    chunks = [(at, min(256, key_count - at)) for at in range(0, key_count, 256)]

    for tile in range(queries.shape[1] // row_tile):
        rows = slice(tile * row_tile, (tile + 1) * row_tile)
        query_tile = queries[0, rows]
        highest = None
        for at, width in chunks:
            scores = lax.dot_general(
                query_tile,
                key_buffer[at : at + width],
                (((1,), (1,)), ((), ())),
                preferred_element_type=jnp.float32,
            )
            seen = bias[0, tile * groups : (tile + 1) * groups, base + at : base + at + width]
            scores = scores.reshape(groups, block_rows, width) + seen[:, None, :]
            scores = scores.reshape(row_tile, width)
            score_buffer[:, at : at + width] = scores
            for place in range(0, width, 128):
                part = scores[:, place : place + 128]
                highest = part if highest is None else jnp.maximum(highest, part)
        top = jnp.max(highest, axis=1, keepdims=True)
        if not first:
            top = jnp.maximum(top, marks_in[0, rows, :1])
        total = jnp.zeros((row_tile, 128), jnp.float32)
        summed = jnp.zeros((row_tile, head_dim), jnp.float32)
        for at, width in chunks:
            weights = jnp.exp2((score_buffer[:, at : at + width] - top) * factor)
            for place in range(0, width, 128):
                total = total + weights[:, place : place + 128]
            summed = summed + jnp.dot(
                weights.astype(jnp.bfloat16),
                value_buffer[at : at + width],
                preferred_element_type=jnp.float32,
            )
        total = jnp.sum(total, axis=1, keepdims=True)
        if not first:
            shrink = jnp.exp2((marks_in[0, rows, :1] - top) * factor)
            total = total + shrink * marks_in[0, rows, 127:]
            summed = summed + shrink * sum_in[0, rows]
        if last:
            outs[0][0, rows] = (summed / total).astype(jnp.bfloat16)
        else:
            lane = lax.broadcasted_iota(jnp.int32, (row_tile, 128), 1)
            outs[0][0, rows] = jnp.where(lane < 64, top, total)
            outs[1][0, rows] = summed


def attend(queries, bias, span, shifts, arrays, pieces, state, last, block_rows):
    slots, slot_rows, head_dim = queries.shape
    key_count = span[1] - span[0]
    slot_spec = pl.BlockSpec((1, slot_rows, head_dim), lambda s, *_: (s, 0, 0))
    specs = [slot_spec, pl.BlockSpec((1,) + bias.shape[1:], lambda s, *_: (s, 0, 0))]
    for which, array in enumerate(arrays):
        own = any(kind == "own" for w, kind, index in pieces if w == which)
        if own:
            specs.append(pl.BlockSpec((1,) + array.shape[1:], lambda s, *_: (s, 0, 0, 0, 0)))
        else:
            specs.append(pl.BlockSpec(array.shape, lambda s, *_: (0, 0, 0, 0, 0)))
    state_shape = jax.ShapeDtypeStruct((slots, slot_rows, 128), jnp.float32)
    if last:
        out_shape = [jax.ShapeDtypeStruct(queries.shape, jnp.bfloat16)]
    else:
        out_shape = [state_shape] * 2
    carried = [] if state is None else list(state)
    specs += [slot_spec] * len(carried)
    plan = {"arrays": len(arrays), "pieces": pieces, "base": span[0]}
    return pl.pallas_call(
        functools.partial(attend_kernel, plan, state is None, last, block_rows),
        out_shape=out_shape,
        grid_spec=pltpu.PrefetchScalarGridSpec(
            num_scalar_prefetch=1,
            grid=(slots,),
            in_specs=specs,
            out_specs=[slot_spec] * len(out_shape),
            scratch_shapes=[
                pltpu.VMEM((key_count, head_dim), jnp.bfloat16),
                pltpu.VMEM((key_count, head_dim), jnp.bfloat16),
                pltpu.VMEM((row_tile, key_count), jnp.float32),
            ],
        ),
        cost_estimate=pl.CostEstimate(
            flops=4 * slots * slot_rows * key_count * head_dim,
            transcendentals=slots * slot_rows * key_count,
            bytes_accessed=8 * 1024 * 1024,
        ),
    )(shifts, queries, bias, *arrays, *carried)


def after(value, *earlier):
    return lax.optimization_barrier((value,) + earlier)[0]


def local(queries, keys, values, block_mask, strides, offsets):
    core = lax.axis_index("core")
    plane = lax.axis_index("x")
    depth = lax.axis_index("z")
    cores, depths, planes = lax.axis_size("core"), lax.axis_size("z"), lax.axis_size("x")
    frame_total, frame_blocks = block_mask.shape[0], block_mask.shape[1]
    local_rows, _, head_dim = queries.shape
    rows_y = lax.axis_size("y")
    block_rows = local_rows * rows_y * cores // frame_blocks
    halves = local_rows // block_rows
    swap = [(0, 1), (1, 0)]

    def spread(packed):
        return lax.all_to_all(packed, ("x", "y"), split_axis=0, concat_axis=0, tiled=True)

    def onward(carried, distance):
        route = [(z, (z + distance) % depths) for z in range(depths)]
        route += [(depths + z, depths + (z - distance) % depths) for z in range(depths)]
        return lax.ppermute(carried, ("core", "z"), route)

    anchors = (frame_blocks - offsets % frame_blocks) % frame_blocks
    residue = lax.dynamic_index_in_dim(anchors, plane * depths + depth, keepdims=False) % 4
    packed = jnp.stack([jnp.transpose(keys, (1, 0, 2)), jnp.transpose(values, (1, 0, 2))], axis=1)
    block = lax.dynamic_slice_in_dim(packed, (residue % 2) * block_rows, block_rows, axis=2)
    block = jnp.where(residue // 2 == core, block, lax.ppermute(block, "core", swap))
    block = spread(block)

    slot_ids = jnp.arange(planes, dtype=jnp.int32)
    own_frames = slot_ids * depths + depth
    own_anchors = lax.dynamic_index_in_dim(
        anchors.reshape(planes, depths), depth, 1, keepdims=False
    )
    parts = jnp.arange(4, dtype=jnp.int32)
    parts = parts * 2 - 3 * (parts // 2)
    row_y = (own_anchors[:, None] // 4 + parts[None, :]) % 4
    index = (slot_ids[:, None] * rows_y + row_y).reshape(-1)
    held = jnp.take(block, index, axis=0).reshape(planes, 4, 2, block_rows, head_dim)

    head_queries = spread(after(jnp.transpose(queries, (1, 0, 2)), held))
    own_pair = spread(after(packed, head_queries))
    head_queries = head_queries.reshape(planes, rows_y * local_rows, head_dim)
    own_pair = own_pair.reshape(planes, rows_y, 2, local_rows, head_dim)
    partner_pair = lax.ppermute(own_pair, "core", swap)

    own_mask = lax.dynamic_index_in_dim(
        block_mask.reshape(planes, depths, frame_blocks, frame_blocks), depth, 1, keepdims=False
    )
    split_mask = own_mask.reshape(planes, rows_y, cores, halves, frame_blocks)
    query_mask = lax.dynamic_index_in_dim(split_mask, core, 2, keepdims=False)
    query_mask = query_mask.reshape(planes, -1, frame_blocks).astype(jnp.bfloat16)
    near_steps = lax.iota(jnp.int32, 6) % 3 + 1
    near_signs = (1 - 2 * (lax.iota(jnp.int32, 6) // 3)) * (2 * core - 1)
    shifts = (depth + near_signs * near_steps) // depths + planes

    calls, entries = [], []

    def begin():
        calls.append(([], [], [len(entries)]))

    def end():
        while len(entries) % 2:
            entries.append((3, 1, 0, 0, 0))
        calls[-1][2].append(len(entries))

    def anchor(which, entry, side, distance):
        calls[-1][1].append((which, "anchor", entry))
        entries.extend((2, side, distance, 0, place) for place in range(planes))

    def extra(which, entry, side, distance, part):
        shift = (0 if side == 1 else 3) + distance - 1
        calls[-1][1].append((which, "extra", (shift, entry)))
        entries.append((1, side, distance, part, 0))

    def own(which, partner):
        calls[-1][1].append((which, "own", None))
        spacing = frame_blocks // rows_y
        for y in range(rows_y):
            entries.extend((0, 1, 0, partner, spacing * y + j) for j in range(halves))

    def first_pieces(which, entry, side):
        anchor(which, entry, side, 1)
        extra(which, entry + 1, side, 1, 2)
        extra(which, entry + 2, side, 1, 1)
        extra(which, entry + 3, side, 1, 3)

    def second_pieces(which, entry, side):
        anchor(which, entry, side, 2)
        anchor(which, entry + 2, side, 3)
        extra(which, entry + 1, side, 2, 2)
        extra(which, entry + 3, side, 3, 2)

    begin()
    anchor(0, 0, 1, 0)
    first_pieces(1, 0, 1)
    end()
    begin()
    second_pieces(0, 0, 1)
    first_pieces(1, 0, -1)
    second_pieces(1, 4, -1)
    end()
    begin()
    own(0, 0)
    own(1, 1)
    for entry in range(3):
        anchor(2, entry, 1, 4 + entry)
    end()
    begin()
    for entry in range(2):
        anchor(0, entry, 1, 7 + entry)
    end()
    begin()
    for entry in range(4):
        anchor(0, entry, -1, 4 + entry)
    end()

    table = jnp.asarray(np.array(entries, np.int32).T)
    kind, side, distance, part, place = (table[row][None, :] for row in range(5))
    sign = (2 * core - 1) * side
    near = own_frames[:, None] + sign * distance
    far = place * depths + (depth + sign * distance + depths) % depths
    source = jnp.where(kind == 1, near, far)
    stride = jnp.where(distance == 1, strides[1], jnp.where(distance == 2, strides[2], strides[3]))
    fits = (near >= 0) & (near < frame_total) & ((4 * part) % stride == 0)
    valid = jnp.where(kind == 1, fits, source != own_frames[:, None])
    valid = (valid | (kind == 0)) & (kind != 3)
    every = jnp.arange(frame_total, dtype=jnp.int32)
    picked = jnp.where(source[:, :, None] == every, anchors, 0)
    column = (jnp.sum(picked, axis=2) + 4 * part) % frame_blocks
    column = jnp.where(kind == 0, place + halves * (core ^ part), column)
    code = jnp.repeat(jnp.where(valid, column, -1), block_rows, axis=1)
    chosen = jnp.arange(frame_blocks, dtype=jnp.int32)[None, :, None] == code[:, None, :]
    kept = jnp.einsum(
        "sbc,scn->sbn",
        query_mask,
        chosen.astype(jnp.bfloat16),
        preferred_element_type=jnp.float32,
    )
    bias = jnp.where(kept > 0.5, 0.0, masked_score)

    def run(number, arrays, state, last=False):
        pieces, (start, stop) = calls[number][1:]
        span = (start * block_rows, stop * block_rows)
        return attend(
            head_queries, bias, span, shifts, arrays, pieces, state, last, block_rows
        )

    first = onward(held, 1)
    second = onward(jnp.concatenate([held[:, :2], first[:, :2]], axis=1), 2)
    third = onward(
        jnp.concatenate([first[:, :1], second[:, :1], second[:, 2:3]], axis=1), 3
    )
    fourth = onward(third[:, :2], 3)
    near_other = lax.ppermute(jnp.concatenate([first, second], axis=1), "core", swap)
    far_other = lax.ppermute(
        jnp.concatenate([third, fourth[:, :1]], axis=1), "core", swap
    )
    state = run(0, [held[:, :1], first], None)
    state = run(1, [second, near_other], state)
    state = run(2, [own_pair, partner_pair, third], state)
    state = run(3, [fourth], state)
    state = run(4, [far_other], state, last=True)

    output = state[0].reshape(planes * rows_y, local_rows, head_dim)
    return jnp.transpose(spread(output), (1, 0, 2))


def solution(mesh):
    grid = Mesh(mesh.devices.reshape(4, 2, 4, 16), ("y", "core", "x", "z"))
    tokens = P(("x", "z", "y", "core"), None, None)
    return jax.shard_map(
        local,
        mesh=grid,
        in_specs=(tokens, tokens, tokens, P(), P(), P()),
        out_specs=tokens,
        check_vma=False,
    )
```

```python
import functools

import jax
import jax.numpy as jnp
import numpy as np
from jax import lax
from jax.experimental import pallas as pl
from jax.experimental.pallas import tpu as pltpu
from jax.sharding import Mesh
from jax.sharding import PartitionSpec as P


masked_score = -1e30
log2_e = 1.4426950408889634
row_tile = 256


def attend_kernel(plan, first, last, block_rows, shifts, queries, bias, *refs):
    arrays = refs[: plan["arrays"]]
    refs = refs[plan["arrays"] :]
    if not first:
        marks_in, sum_in = refs[:2]
        refs = refs[2:]
    outs, (key_buffer, value_buffer, score_buffer) = refs[:-3], refs[-3:]
    slot = pl.program_id(0)

    def fill(part):
        position = 0
        for which, kind, index in plan["pieces"]:
            source = arrays[which]
            head_dim = source.shape[4]
            if kind == "own":
                size = source.shape[1] * source.shape[3]
                if part == "slot":
                    shape = (size, head_dim)
                    key_buffer[position : position + size] = source[0, :, 0].reshape(shape)
                    value_buffer[position : position + size] = source[0, :, 1].reshape(shape)
            elif kind == "extra":
                size = block_rows
                if part == "slot":
                    shift, entry = index
                    place = (slot + shifts[shift]) & 3
                    key_buffer[position : position + size] = source[place, entry, 0]
                    value_buffer[position : position + size] = source[place, entry, 1]
            else:
                size = source.shape[0] * block_rows
                if part == "once":
                    shape = (size, head_dim)
                    key_buffer[position : position + size] = source[:, index, 0].reshape(shape)
                    value_buffer[position : position + size] = source[:, index, 1].reshape(shape)
            position += size
        spare = key_buffer.shape[0] - position
        if part == "once" and spare:
            key_buffer[position:] = jnp.zeros((spare, key_buffer.shape[1]), jnp.bfloat16)
            value_buffer[position:] = jnp.zeros((spare, key_buffer.shape[1]), jnp.bfloat16)

    @pl.when(slot == 0)
    def _():
        fill("once")

    if any(kind != "anchor" for _, kind, _ in plan["pieces"]):
        fill("slot")

    key_count, head_dim = key_buffer.shape
    factor = head_dim ** (-0.5) * log2_e
    groups = row_tile // block_rows
    base = plan["base"]
    chunks = [(at, min(256, key_count - at)) for at in range(0, key_count, 256)]

    for tile in range(queries.shape[1] // row_tile):
        rows = slice(tile * row_tile, (tile + 1) * row_tile)
        query_tile = queries[0, rows]
        highest = None
        for at, width in chunks:
            scores = lax.dot_general(
                query_tile,
                key_buffer[at : at + width],
                (((1,), (1,)), ((), ())),
                preferred_element_type=jnp.float32,
            )
            seen = bias[0, tile * groups : (tile + 1) * groups, base + at : base + at + width]
            scores = scores.reshape(groups, block_rows, width) + seen[:, None, :]
            scores = scores.reshape(row_tile, width)
            score_buffer[:, at : at + width] = scores
            for place in range(0, width, 128):
                part = scores[:, place : place + 128]
                highest = part if highest is None else jnp.maximum(highest, part)
        top = jnp.max(highest, axis=1, keepdims=True)
        if not first:
            top = jnp.maximum(top, marks_in[0, rows, :1])
        total = jnp.zeros((row_tile, 128), jnp.float32)
        summed = jnp.zeros((row_tile, head_dim), jnp.float32)
        for at, width in chunks:
            weights = jnp.exp2((score_buffer[:, at : at + width] - top) * factor)
            for place in range(0, width, 128):
                total = total + weights[:, place : place + 128]
            summed = summed + jnp.dot(
                weights.astype(jnp.bfloat16),
                value_buffer[at : at + width],
                preferred_element_type=jnp.float32,
            )
        total = jnp.sum(total, axis=1, keepdims=True)
        if not first:
            shrink = jnp.exp2((marks_in[0, rows, :1] - top) * factor)
            total = total + shrink * marks_in[0, rows, 127:]
            summed = summed + shrink * sum_in[0, rows]
        if last:
            outs[0][0, rows] = (summed / total).astype(jnp.bfloat16)
        else:
            lane = lax.broadcasted_iota(jnp.int32, (row_tile, 128), 1)
            outs[0][0, rows] = jnp.where(lane < 64, top, total)
            outs[1][0, rows] = summed


def attend(queries, bias, span, shifts, arrays, pieces, state, last, block_rows):
    slots, slot_rows, head_dim = queries.shape
    key_count = span[1] - span[0]
    slot_spec = pl.BlockSpec((1, slot_rows, head_dim), lambda s, *_: (s, 0, 0))
    specs = [slot_spec, pl.BlockSpec((1,) + bias.shape[1:], lambda s, *_: (s, 0, 0))]
    for which, array in enumerate(arrays):
        own = any(kind == "own" for w, kind, index in pieces if w == which)
        if own:
            specs.append(pl.BlockSpec((1,) + array.shape[1:], lambda s, *_: (s, 0, 0, 0, 0)))
        else:
            specs.append(pl.BlockSpec(array.shape, lambda s, *_: (0, 0, 0, 0, 0)))
    state_shape = jax.ShapeDtypeStruct((slots, slot_rows, 128), jnp.float32)
    if last:
        out_shape = [jax.ShapeDtypeStruct(queries.shape, jnp.bfloat16)]
    else:
        out_shape = [state_shape] * 2
    carried = [] if state is None else list(state)
    specs += [slot_spec] * len(carried)
    plan = {"arrays": len(arrays), "pieces": pieces, "base": span[0]}
    return pl.pallas_call(
        functools.partial(attend_kernel, plan, state is None, last, block_rows),
        out_shape=out_shape,
        grid_spec=pltpu.PrefetchScalarGridSpec(
            num_scalar_prefetch=1,
            grid=(slots,),
            in_specs=specs,
            out_specs=[slot_spec] * len(out_shape),
            scratch_shapes=[
                pltpu.VMEM((key_count, head_dim), jnp.bfloat16),
                pltpu.VMEM((key_count, head_dim), jnp.bfloat16),
                pltpu.VMEM((row_tile, key_count), jnp.float32),
            ],
        ),
        cost_estimate=pl.CostEstimate(
            flops=4 * slots * slot_rows * key_count * head_dim,
            transcendentals=slots * slot_rows * key_count,
            bytes_accessed=8 * 1024 * 1024,
        ),
    )(shifts, queries, bias, *arrays, *carried)


def after(value, *earlier):
    return lax.optimization_barrier((value,) + earlier)[0]


def local(queries, keys, values, block_mask, strides, offsets):
    core = lax.axis_index("core")
    plane = lax.axis_index("x")
    depth = lax.axis_index("z")
    cores, depths, planes = lax.axis_size("core"), lax.axis_size("z"), lax.axis_size("x")
    frame_total, frame_blocks = block_mask.shape[0], block_mask.shape[1]
    local_rows, _, head_dim = queries.shape
    rows_y = lax.axis_size("y")
    block_rows = local_rows * rows_y * cores // frame_blocks
    halves = local_rows // block_rows
    swap = [(0, 1), (1, 0)]

    def spread(packed):
        return lax.all_to_all(packed, ("x", "y"), split_axis=0, concat_axis=0, tiled=True)

    def onward(carried, distance):
        route = [(z, (z + distance) % depths) for z in range(depths)]
        route += [(depths + z, depths + (z - distance) % depths) for z in range(depths)]
        return lax.ppermute(carried, ("core", "z"), route)

    anchors = (frame_blocks - offsets % frame_blocks) % frame_blocks
    residue = lax.dynamic_index_in_dim(anchors, plane * depths + depth, keepdims=False) % 4
    packed = jnp.stack([jnp.transpose(keys, (1, 0, 2)), jnp.transpose(values, (1, 0, 2))], axis=1)
    block = lax.dynamic_slice_in_dim(packed, (residue % 2) * block_rows, block_rows, axis=2)
    block = jnp.where(residue // 2 == core, block, lax.ppermute(block, "core", swap))
    block = spread(block)

    slot_ids = jnp.arange(planes, dtype=jnp.int32)
    own_frames = slot_ids * depths + depth
    own_anchors = lax.dynamic_index_in_dim(
        anchors.reshape(planes, depths), depth, 1, keepdims=False
    )
    parts = jnp.arange(4, dtype=jnp.int32)
    parts = parts * 2 - 3 * (parts // 2)
    row_y = (own_anchors[:, None] // 4 + parts[None, :]) % 4
    index = (slot_ids[:, None] * rows_y + row_y).reshape(-1)
    held = jnp.take(block, index, axis=0, mode="clip").reshape(planes, 4, 2, block_rows, head_dim)

    head_queries = spread(after(jnp.transpose(queries, (1, 0, 2)), held))
    own_pair = spread(after(packed, head_queries))
    head_queries = head_queries.reshape(planes, rows_y * local_rows, head_dim)
    own_pair = own_pair.reshape(planes, rows_y, 2, local_rows, head_dim)
    partner_pair = lax.ppermute(own_pair, "core", swap)

    own_mask = lax.dynamic_index_in_dim(
        block_mask.reshape(planes, depths, frame_blocks, frame_blocks), depth, 1, keepdims=False
    )
    split_mask = own_mask.reshape(planes, rows_y, cores, halves, frame_blocks)
    query_mask = lax.dynamic_index_in_dim(split_mask, core, 2, keepdims=False)
    query_mask = query_mask.reshape(planes, -1, frame_blocks).astype(jnp.bfloat16)
    near_steps = lax.iota(jnp.int32, 6) % 3 + 1
    near_signs = (1 - 2 * (lax.iota(jnp.int32, 6) // 3)) * (2 * core - 1)
    shifts = (depth + near_signs * near_steps) // depths + planes

    calls, entries = [], []

    def begin():
        calls.append(([], [], [len(entries)]))

    def end():
        while len(entries) % 2:
            entries.append((3, 1, 0, 0, 0))
        calls[-1][2].append(len(entries))

    def anchor(which, entry, side, distance):
        calls[-1][1].append((which, "anchor", entry))
        entries.extend((2, side, distance, 0, place) for place in range(planes))

    def extra(which, entry, side, distance, part):
        shift = (0 if side == 1 else 3) + distance - 1
        calls[-1][1].append((which, "extra", (shift, entry)))
        entries.append((1, side, distance, part, 0))

    def own(which, partner):
        calls[-1][1].append((which, "own", None))
        spacing = frame_blocks // rows_y
        for y in range(rows_y):
            entries.extend((0, 1, 0, partner, spacing * y + j) for j in range(halves))

    def first_pieces(which, entry, side):
        anchor(which, entry, side, 1)
        extra(which, entry + 1, side, 1, 2)
        extra(which, entry + 2, side, 1, 1)
        extra(which, entry + 3, side, 1, 3)

    def second_pieces(which, entry, side):
        anchor(which, entry, side, 2)
        anchor(which, entry + 2, side, 3)
        extra(which, entry + 1, side, 2, 2)
        extra(which, entry + 3, side, 3, 2)

    begin()
    anchor(0, 0, 1, 0)
    first_pieces(1, 0, 1)
    end()
    begin()
    second_pieces(0, 0, 1)
    first_pieces(1, 0, -1)
    second_pieces(1, 4, -1)
    end()
    begin()
    own(0, 0)
    own(1, 1)
    for which, side in ((2, 1), (3, -1)):
        for entry in range(3):
            anchor(which, entry, side, 4 + entry)
    end()
    begin()
    anchor(0, 0, 1, 7)
    anchor(0, 1, 1, 8)
    anchor(1, 0, -1, 7)
    end()

    table = jnp.asarray(np.array(entries, np.int32).T)
    kind, side, distance, part, place = (table[row][None, :] for row in range(5))
    sign = (2 * core - 1) * side
    near = own_frames[:, None] + sign * distance
    far = place * depths + (depth + sign * distance + depths) % depths
    source = jnp.where(kind == 1, near, far)
    stride = jnp.where(distance == 1, strides[1], jnp.where(distance == 2, strides[2], strides[3]))
    fits = (near >= 0) & (near < frame_total) & ((4 * part) % stride == 0)
    valid = jnp.where(kind == 1, fits, source != own_frames[:, None])
    valid = (valid | (kind == 0)) & (kind != 3)
    every = jnp.arange(frame_total, dtype=jnp.int32)
    picked = jnp.where(source[:, :, None] == every, anchors, 0)
    column = (jnp.sum(picked, axis=2) + 4 * part) % frame_blocks
    column = jnp.where(kind == 0, place + halves * (core ^ part), column)
    code = jnp.repeat(jnp.where(valid, column, -1), block_rows, axis=1)
    chosen = jnp.arange(frame_blocks, dtype=jnp.int32)[None, :, None] == code[:, None, :]
    kept = jnp.einsum(
        "sbc,scn->sbn",
        query_mask,
        chosen.astype(jnp.bfloat16),
        preferred_element_type=jnp.float32,
    )
    bias = jnp.where(kept > 0.5, 0.0, masked_score)

    def run(number, arrays, state, last=False):
        pieces, (start, stop) = calls[number][1:]
        span = (start * block_rows, stop * block_rows)
        return attend(
            head_queries, bias, span, shifts, arrays, pieces, state, last, block_rows
        )

    first = onward(held, 1)
    second = onward(jnp.concatenate([held[:, :2], first[:, :2]], axis=1), 2)
    third = onward(
        jnp.concatenate([first[:, :1], second[:, :1], second[:, 2:3]], axis=1), 3
    )
    fourth = onward(third[:, :2], 3)
    near_other = lax.ppermute(jnp.concatenate([first, second], axis=1), "core", swap)
    third_other = lax.ppermute(third, "core", swap)
    fourth_other = lax.ppermute(fourth[:, :1], "core", swap)
    state = run(0, [held, first], None)
    state = run(1, [second, near_other], state)
    state = run(2, [own_pair, partner_pair, third, third_other], state)
    state = run(3, [fourth, fourth_other], state, last=True)

    output = state[0].reshape(planes * rows_y, local_rows, head_dim)
    return jnp.transpose(spread(output), (1, 0, 2))


def solution(mesh):
    grid = Mesh(mesh.devices.reshape(4, 2, 4, 16), ("y", "core", "x", "z"))
    tokens = P(("x", "z", "y", "core"), None, None)
    return jax.shard_map(
        local,
        mesh=grid,
        in_specs=(tokens, tokens, tokens, P(), P(), P()),
        out_specs=tokens,
        check_vma=False,
    )
```
